32 devices in a mesh: dp: 8 (over z, y), expert: 4 (over x, core).
Axes of the slice: x: 2, y: 2, z: 4, core: 2. Of those that a mesh axis runs over, the one named last changes fastest.
Arguments:
- master_old: float32 [8, 4, 16, 128], P('dp', 'expert'), may hold values from -1.5 to 1.5
- m_codes: bfloat16 [8, 4, 16, 128], P('dp', 'expert'), may hold values from -1 to 1
- m_scale: float32 [8, 4, 16], P('dp', 'expert'), may hold values from 0.05 to 0.5
- v_codes: bfloat16 [8, 4, 16, 128], P('dp', 'expert'), may hold values from 0.049804688 to 1
- v_scale: float32 [8, 4, 16], P('dp', 'expert'), may hold values from 0.1 to 1
- grad_parts: bfloat16 [8, 4, 128, 128], P('dp', 'expert'), may hold values from -100 to 100, as said below
- send_order: int32 [8, 4, 16], P('dp', 'expert'), may hold values from 0 to 15, each once within a row
- recv_place: int32 [8, 4, 16], P('dp', 'expert'), may hold values from 0 to 15, each once within a row
Outputs:
- master_new: float32 [4, 128, 128], P('expert', 'dp')
- m_codes_new: bfloat16 [4, 128, 128], P('expert', 'dp')
- m_scale_new: float32 [4, 128], P('expert', 'dp')
- v_codes_new: bfloat16 [4, 128, 128], P('expert', 'dp')
- v_scale_new: float32 [4, 128], P('expert', 'dp')
The draws below stay inside these ranges and needn't reach their ends.
Inputs may be any that keep to these rules, and one draw needn't show every extreme that they name: `grad_parts`: partial gradients of one data shard.
All inputs are finite; a program needn't handle non-finite values. Where the reference program divides by a largest or mean magnitude, that divisor is 1e-20 or more.
Results may differ from the reference program's by a relative error of at most 0.0004.
Values may be sent and summed in bfloat16 or wider, within the bound.
A program may use at most 64 MiB of HBM per device.

```python
import math
import jax
import jax.numpy as jnp
from jax import lax

BLOCK = 128
BLK_DEV = 16
STEP = 200
SHARD_TOTAL = 8
GROUPS = 4
GROUP_BLK = 128


def draw_grad_parts(key, part):
    key_base = jax.random.fold_in(key, 11)
    key_pair = jax.random.fold_in(key, 12)
    key_common = jax.random.fold_in(key, 13)
    key_group = jax.random.fold_in(key, 14)
    key_share = jax.random.fold_in(key, 15)
    key_rows = jax.random.fold_in(key, 16)
    spike_key = jax.random.fold_in(key, 17)
    shape_all = (SHARD_TOTAL, GROUPS, GROUP_BLK, BLOCK)
    values = jax.random.normal(key_base, shape_all, jnp.float32)
    steepness = 2.0
    row_logarithm = jax.random.uniform(key_rows, (SHARD_TOTAL,), jnp.float32, -1.5, 1.5)
    spike_factor = 2.0
    common = jax.random.normal(key_common, (1, GROUPS, GROUP_BLK, BLOCK), jnp.float32)
    group_scale = jnp.exp(jax.random.uniform(key_group, (GROUPS,), jnp.float32, 0.0, math.log(4.0)))
    group_share = jnp.exp(jax.random.uniform(key_share, (GROUPS,), jnp.float32, math.log(0.25), math.log(4.0)))
    spike_row = jax.random.randint(spike_key, (), 0, SHARD_TOTAL)
    row_position_index = jnp.arange(SHARD_TOTAL)
    row_surplus = jnp.where(row_position_index == spike_row, spike_factor * SHARD_TOTAL, jnp.exp(row_logarithm * math.log(10.0)))
    excess = group_share[:, None] * row_surplus[None, :]
    common_weight = jnp.sqrt(excess / SHARD_TOTAL)
    shard_of = jnp.arange(GROUP_BLK) // BLK_DEV
    weight_rows = common_weight[:, shard_of]
    values = values + weight_rows[None, :, :, None] * common
    rising = 1.0 + steepness * shard_of.astype(jnp.float32) / max(SHARD_TOTAL - 1, 1)
    paired = jax.random.permutation(key_pair, SHARD_TOTAL)
    boost = jnp.where(shard_of[None, :] == paired[:, None], 3.0, 1.0)
    values = values * rising[None, None, :, None] * group_scale[None, :, None, None] * boost[:, None, :, None]
    return jnp.clip(values, -100.0, 100.0).astype(jnp.bfloat16)


def levels(key, extent, shards, least, largest):
    gain = 1.0
    for axis_at, blocks in shards:
        steps = jax.random.uniform(jax.random.fold_in(jax.random.fold_in(key, 6), axis_at), (blocks,), jnp.float32, least / len(shards), largest / len(shards))
        gain = gain * jnp.repeat(jnp.exp(steps), extent[axis_at] // blocks).reshape((-1,) + (1,) * (len(extent) - 1 - axis_at))
    return gain


def noise(own_key, dims, scale, bound, cuts=(), dtype=jnp.bfloat16):
    result = scale * jax.random.normal(own_key, dims, jnp.float32)
    if cuts:
        result = result * levels(own_key, dims, cuts, -0.22, 0.18)
    return jnp.clip(result, -bound, bound).astype(dtype)


def setup_inputs(seed: int = 0) -> dict:
    seeds = jax.random.split(jax.random.key(seed), 9)
    master_old = noise(seeds[0], (SHARD_TOTAL, GROUPS, BLK_DEV, BLOCK), 0.25, 1.5, ((0, 8), (1, 4)), jnp.float32)
    m_codes = jnp.clip(jax.random.uniform(seeds[1], (SHARD_TOTAL, GROUPS, BLK_DEV, BLOCK), jnp.float32, -1.0, 1.0) * levels(seeds[1], (SHARD_TOTAL, GROUPS, BLK_DEV, BLOCK), ((0, 8), (1, 4)), -0.4, 0.0), -1.0, 1.0).astype(jnp.bfloat16)
    m_scale = jnp.clip(jnp.exp(math.log(0.5) - 2.3025851 * jax.random.uniform(seeds[2], (SHARD_TOTAL, GROUPS, BLK_DEV), jnp.float32) ** levels(seeds[2], (SHARD_TOTAL, GROUPS, BLK_DEV), ((0, 8), (1, 4)), -0.2, 0.2)), 0.05, 0.5)
    v_codes = jnp.clip(0.049804688 + 0.9501953 * jax.random.uniform(seeds[3], (SHARD_TOTAL, GROUPS, BLK_DEV, BLOCK), jnp.float32) ** levels(seeds[3], (SHARD_TOTAL, GROUPS, BLK_DEV, BLOCK), ((0, 8), (1, 4)), -0.2, 0.2), 0.049804688, 1.0).astype(jnp.bfloat16)
    v_scale = jnp.clip(jnp.exp(math.log(1.0) - 2.3025851 * jax.random.uniform(seeds[4], (SHARD_TOTAL, GROUPS, BLK_DEV), jnp.float32) ** levels(seeds[4], (SHARD_TOTAL, GROUPS, BLK_DEV), ((0, 8), (1, 4)), -0.2, 0.2)), 0.1, 1.0)
    grad_parts = draw_grad_parts(jax.random.fold_in(seeds[8], 71), 0)
    send_order = jax.vmap(lambda own: jax.random.permutation(own, BLK_DEV))(jax.random.split(seeds[6], SHARD_TOTAL * GROUPS)).reshape((SHARD_TOTAL, GROUPS, BLK_DEV)).astype(jnp.int32)
    recv_place = jax.vmap(lambda own: jax.random.permutation(own, BLK_DEV))(jax.random.split(seeds[7], SHARD_TOTAL * GROUPS)).reshape((SHARD_TOTAL, GROUPS, BLK_DEV)).astype(jnp.int32)
    return dict(master_old=master_old, m_codes=m_codes, m_scale=m_scale, v_codes=v_codes, v_scale=v_scale, grad_parts=grad_parts, send_order=send_order, recv_place=recv_place)


BETA_ONE = 0.9
BETA_TWO = 0.999
ADAM_EPS = 1e-08
LEARN_RATE = 0.05
DECAY_RATE = 0.1
CLIP_RMS = 1.0
QUANT_EPS = 1e-06
NORM_EPS = 1e-06

def dequant(codes, scales):
    return codes.astype(jnp.float32) * scales[..., None]

def requant(moment):
    magnitude = lax.optimization_barrier(jnp.max(jnp.abs(moment), axis=-1)) + QUANT_EPS
    return ((moment / magnitude[..., None]).astype(jnp.bfloat16), magnitude)

def widen_index(order, values):
    extra = values.ndim - 3
    shaped = order.reshape(order.shape + (1,) * extra)
    return jnp.broadcast_to(shaped, order.shape + values.shape[3:])

def relay_blocks(values, send_order, recv_place):
    shard_count, group_count, block_count = send_order.shape
    slot_size = block_count // group_count
    picked = jnp.take_along_axis(values, widen_index(send_order, values), axis=2)
    picked = picked.reshape((shard_count, group_count, group_count, slot_size) + values.shape[3:])
    arrived = jnp.swapaxes(picked, 1, 2).reshape(values.shape)
    inverse = jnp.argsort(recv_place, axis=-1).astype(jnp.int32)
    placed = jnp.take_along_axis(arrived, widen_index(inverse, arrived), axis=2)
    placed = jnp.swapaxes(placed, 0, 1)
    return placed.reshape((group_count, shard_count * block_count) + values.shape[3:])

def reference(master_old, m_codes, m_scale, v_codes, v_scale, grad_parts, send_order, recv_place):
    master = relay_blocks(master_old, send_order, recv_place)
    moment_one = relay_blocks(dequant(m_codes, m_scale), send_order, recv_place)
    moment_two = relay_blocks(dequant(v_codes, v_scale), send_order, recv_place)

    def accumulate(total, piece):
        return (total + piece.astype(jnp.float32), None)
    gradient, unused_out = lax.scan(accumulate, jnp.zeros(grad_parts.shape[1:], jnp.float32), grad_parts)
    total_squares = jnp.sum(gradient * gradient)
    root_mean = jnp.sqrt(total_squares / gradient.size + NORM_EPS)
    clip_factor = jnp.minimum(1.0, CLIP_RMS / root_mean)
    clipped = clip_factor * gradient
    m_next = BETA_ONE * moment_one + (1.0 - BETA_ONE) * clipped
    v_next = BETA_TWO * moment_two + (1.0 - BETA_TWO) * clipped * clipped
    bias_one = 1.0 - BETA_ONE ** STEP
    bias_two = 1.0 - BETA_TWO ** STEP
    update = m_next / bias_one / (jnp.sqrt(v_next / bias_two) + ADAM_EPS)
    master_new = master - LEARN_RATE * (update + DECAY_RATE * master)
    m_codes_new, m_scale_new = requant(m_next)
    v_codes_new, v_scale_new = requant(v_next)
    return (master_new, m_codes_new, m_scale_new, v_codes_new, v_scale_new)
```

```python
import functools

import jax
import jax.numpy as jnp
from jax import lax
from jax.experimental import pallas as pl
from jax.experimental.pallas import tpu as pltpu
from jax.sharding import PartitionSpec as P

STEP = 200

BETA_ONE = 0.9
BETA_TWO = 0.999
ADAM_EPS = 1e-08
LEARN_RATE = 0.05
DECAY_RATE = 0.1
CLIP_RMS = 1.0
QUANT_EPS = 1e-06
NORM_EPS = 1e-06

MESH = pl.DeviceIdType.MESH
UNROLL = 40


def each(first, last, step):
    if last - first <= UNROLL:
        for k in range(first, last):
            step(k)
    else:
        lax.fori_loop(first, last, lambda k, c: (step(k), c)[1], 0)


def kernel(
    shards, groups,
    master_in, mc_in, ms_in, vc_in, vs_in, grads_in, order_in, place_in,
    master_out, mc_out, ms_out, vc_out, vs_out,
    master_v, mc_v, vc_v, grads_v, m_wide, v_wide,
    ms_s, vs_s, order_s, place_s,
    relay_out, relay_in, grad_in, square_out, square_in,
    in_sems, grad_sems, relay_sems, square_sems,
):
    d = lax.axis_index("dp")
    e = lax.axis_index("expert")
    blocks, block = master_v.shape
    q = blocks // groups
    total = shards * groups

    barrier = pltpu.get_barrier_semaphore()

    def greet_shard(k):
        pl.semaphore_signal(barrier, inc=1, device_id=(lax.rem(d + k, shards), e), device_id_type=MESH)

    def greet_group(k):
        pl.semaphore_signal(barrier, inc=1, device_id=(d, lax.rem(e + k, groups)), device_id_type=MESH)

    each(1, shards, greet_shard)
    each(1, groups, greet_group)

    loads = [
        pltpu.make_async_copy(src, dst, in_sems.at[i])
        for i, (src, dst) in enumerate((
            (grads_in, grads_v), (order_in, order_s), (ms_in, ms_s), (vs_in, vs_s),
            (mc_in, mc_v), (vc_in, vc_v), (master_in, master_v), (place_in, place_s),
        ))
    ]
    for load in loads:
        load.start()
    loads[0].wait()
    pl.semaphore_wait(barrier, shards - 1 + groups - 1)

    def grad_copy(k):
        to = lax.rem(d + k, shards)
        return pltpu.make_async_remote_copy(
            src_ref=grads_v.at[to], dst_ref=grad_in.at[k - 1],
            send_sem=grad_sems.at[0], recv_sem=grad_sems.at[1],
            device_id=(to, e), device_id_type=MESH)

    each(1, shards, lambda k: grad_copy(k).start())

    for load in loads[1:]:
        load.wait()
    m_wide[...] = mc_v[...].astype(jnp.float32)
    v_wide[...] = vc_v[...].astype(jnp.float32)

    def relay_copy(k):
        to = lax.rem(e + k, groups)
        return pltpu.make_async_remote_copy(
            src_ref=relay_out.at[k], dst_ref=relay_in.at[k - 1],
            send_sem=relay_sems.at[0], recv_sem=relay_sems.at[1],
            device_id=(d, to), device_id_type=MESH)

    for k in list(range(1, groups)) + [0]:
        to = lax.rem(e + k, groups)
        for c in range(q):
            row = order_s[0, to * q + c]
            relay_out[k, 0, c : c + 1, :] = master_v[pl.ds(row, 1), :]
            relay_out[k, 1, c : c + 1, :] = m_wide[pl.ds(row, 1), :] * ms_s[0, row]
            relay_out[k, 2, c : c + 1, :] = v_wide[pl.ds(row, 1), :] * vs_s[0, row]
        if k:
            relay_copy(k).start()

    whole = pltpu.make_async_remote_copy(
        src_ref=grad_in, dst_ref=grad_in, send_sem=grad_sems.at[0], recv_sem=grad_sems.at[1],
        device_id=(lax.rem(d + 1, shards), e), device_id_type=MESH)
    whole.wait_recv()
    gradient = grads_v[d].astype(jnp.float32)
    if shards - 1 <= UNROLL:
        for k in range(shards - 1):
            gradient = gradient + grad_in[k].astype(jnp.float32)
    else:
        gradient = lax.fori_loop(
            0, shards - 1, lambda k, g: g + grad_in[k].astype(jnp.float32), gradient)
    squares = jnp.sum(gradient * gradient, axis=0, keepdims=True)
    square_out[...] = squares

    def square_copy(k):
        flat = lax.rem(d * groups + e + k, total)
        return pltpu.make_async_remote_copy(
            src_ref=square_out, dst_ref=square_in.at[k - 1],
            send_sem=square_sems.at[0], recv_sem=square_sems.at[1],
            device_id=(flat // groups, lax.rem(flat, groups)), device_id_type=MESH)

    each(1, total, lambda k: square_copy(k).start())

    relay_whole = pltpu.make_async_remote_copy(
        src_ref=relay_in, dst_ref=relay_in, send_sem=relay_sems.at[0], recv_sem=relay_sems.at[1],
        device_id=(d, lax.rem(e + 1, groups)), device_id_type=MESH)
    relay_whole.wait_recv()
    rows = lax.broadcasted_iota(jnp.int32, (blocks, block), 0)
    placed = [jnp.zeros((blocks, block), jnp.float32) for _ in range(3)]
    for k in range(groups):
        frm = lax.rem(e - k + groups, groups)
        for c in range(q):
            here = rows == place_s[0, frm * q + c]
            for i in range(3):
                row = relay_out[0, i, c : c + 1, :] if k == 0 else relay_in[k - 1, i, c : c + 1, :]
                placed[i] = jnp.where(here, jnp.broadcast_to(row, (blocks, block)), placed[i])
    master, moment_one, moment_two = placed

    square_whole = pltpu.make_async_remote_copy(
        src_ref=square_in, dst_ref=square_in, send_sem=square_sems.at[0], recv_sem=square_sems.at[1],
        device_id=(lax.rem(d + 1, shards), e), device_id_type=MESH)
    square_whole.wait_recv()
    lanes = jnp.sum(square_in[...], axis=0) + squares
    total_squares = jnp.sum(lanes, axis=1, keepdims=True)
    root_mean = jnp.sqrt(total_squares / (total * blocks * block) + NORM_EPS)
    clip_factor = jnp.minimum(1.0, CLIP_RMS / root_mean)

    clipped = clip_factor * gradient
    m_next = BETA_ONE * moment_one + (1.0 - BETA_ONE) * clipped
    v_next = BETA_TWO * moment_two + (1.0 - BETA_TWO) * clipped * clipped
    bias_one = 1.0 - BETA_ONE**STEP
    bias_two = 1.0 - BETA_TWO**STEP
    m_mag = jnp.max(jnp.abs(m_next), axis=1, keepdims=True) + QUANT_EPS
    v_mag = jnp.max(jnp.abs(v_next), axis=1, keepdims=True) + QUANT_EPS
    update = m_next / bias_one / (jnp.sqrt(v_next / bias_two) + ADAM_EPS)
    master_out[...] = master - LEARN_RATE * (update + DECAY_RATE * master)
    mc_out[...] = (m_next / m_mag).astype(jnp.bfloat16)
    vc_out[...] = (v_next / v_mag).astype(jnp.bfloat16)
    diagonal = rows == lax.broadcasted_iota(jnp.int32, (blocks, block), 1)
    ms_out[...] = jnp.sum(jnp.where(diagonal, m_mag, 0.0), axis=0, keepdims=True)[:, :blocks]
    vs_out[...] = jnp.sum(jnp.where(diagonal, v_mag, 0.0), axis=0, keepdims=True)[:, :blocks]

    whole.wait_send()
    relay_whole.wait_send()
    square_whole.wait_send()


def body(shards, groups, master_old, m_codes, m_scale, v_codes, v_scale, grad_parts, send_order, recv_place):
    blocks, block = master_old.shape[2:]
    q = blocks // groups
    f32, bf16 = jnp.float32, jnp.bfloat16
    wide = (blocks, block)
    anywhere = pl.BlockSpec(memory_space=pl.ANY)
    vmem = pl.BlockSpec(memory_space=pltpu.VMEM)
    master_new, mc, ms, vc, vs = pl.pallas_call(
        functools.partial(kernel, shards, groups),
        out_shape=(
            jax.ShapeDtypeStruct(wide, f32),
            jax.ShapeDtypeStruct(wide, bf16),
            jax.ShapeDtypeStruct((1, blocks), f32),
            jax.ShapeDtypeStruct(wide, bf16),
            jax.ShapeDtypeStruct((1, blocks), f32),
        ),
        in_specs=[anywhere] * 8,
        out_specs=(vmem,) * 5,
        scratch_shapes=[
            pltpu.VMEM(wide, f32),
            pltpu.VMEM(wide, bf16),
            pltpu.VMEM(wide, bf16),
            pltpu.VMEM((shards, blocks, block), bf16),
            pltpu.VMEM(wide, f32),
            pltpu.VMEM(wide, f32),
            pltpu.SMEM((1, blocks), f32),
            pltpu.SMEM((1, blocks), f32),
            pltpu.SMEM((1, blocks), jnp.int32),
            pltpu.SMEM((1, blocks), jnp.int32),
            pltpu.VMEM((groups, 3, q, block), f32),
            pltpu.VMEM((groups - 1, 3, q, block), f32),
            pltpu.VMEM((shards - 1, blocks, block), bf16),
            pltpu.VMEM((1, block), f32),
            pltpu.VMEM((shards * groups - 1, 1, block), f32),
            pltpu.SemaphoreType.DMA((8,)),
            pltpu.SemaphoreType.DMA((2,)),
            pltpu.SemaphoreType.DMA((2,)),
            pltpu.SemaphoreType.DMA((2,)),
        ],
        compiler_params=pltpu.CompilerParams(collective_id=0, has_side_effects=True),
    )(
        master_old.reshape(wide), m_codes.reshape(wide), m_scale.reshape(1, blocks),
        v_codes.reshape(wide), v_scale.reshape(1, blocks),
        grad_parts.reshape(shards, blocks, block),
        send_order.reshape(1, blocks), recv_place.reshape(1, blocks),
    )
    return master_new[None], mc[None], ms, vc[None], vs


def solution(mesh):
    rows = P("dp", "expert", None, None)
    flat = P("dp", "expert", None)
    return jax.shard_map(
        functools.partial(body, mesh.shape["dp"], mesh.shape["expert"]),
        mesh=mesh,
        in_specs=(rows, rows, flat, rows, flat, rows, flat, flat),
        out_specs=(
            P("expert", "dp", None),
            P("expert", "dp", None),
            P("expert", "dp"),
            P("expert", "dp", None),
            P("expert", "dp"),
        ),
        check_vma=False,
    )
```

```python
import functools

import jax
import jax.numpy as jnp
from jax import lax
from jax.experimental import pallas as pl
from jax.experimental.pallas import tpu as pltpu
from jax.sharding import PartitionSpec as P

STEP = 200

BETA_ONE = 0.9
BETA_TWO = 0.999
ADAM_EPS = 1e-08
LEARN_RATE = 0.05
DECAY_RATE = 0.1
CLIP_RMS = 1.0
QUANT_EPS = 1e-06
NORM_EPS = 1e-06

MESH = pl.DeviceIdType.MESH
UNROLL = 40


def each(first, last, step):
    if last - first <= UNROLL:
        for k in range(first, last):
            step(k)
    else:
        lax.fori_loop(first, last, lambda k, c: (step(k), c)[1], 0)


def kernel(
    shards, groups,
    master_in, mc_in, ms_in, vc_in, vs_in, grads_in, order_in, place_in,
    state_out, lanes_out,
    master_v, mc_v, vc_v, grads_v, m_wide, v_wide,
    ms_s, vs_s, order_s, place_s,
    relay_out, relay_in, grad_in, square_out, square_in,
    in_sems, grad_sems, relay_sems, square_sems,
):
    d = lax.axis_index("dp")
    e = lax.axis_index("expert")
    blocks, block = master_v.shape
    q = blocks // groups
    total = shards * groups

    barrier = pltpu.get_barrier_semaphore()

    def greet_shard(k):
        pl.semaphore_signal(barrier, inc=1, device_id=(lax.rem(d + k, shards), e), device_id_type=MESH)

    def greet_group(k):
        pl.semaphore_signal(barrier, inc=1, device_id=(d, lax.rem(e + k, groups)), device_id_type=MESH)

    each(1, shards, greet_shard)
    each(1, groups, greet_group)

    loads = [
        pltpu.make_async_copy(src, dst, in_sems.at[i])
        for i, (src, dst) in enumerate((
            (grads_in, grads_v), (order_in, order_s), (ms_in, ms_s), (vs_in, vs_s),
            (mc_in, mc_v), (vc_in, vc_v), (master_in, master_v), (place_in, place_s),
        ))
    ]
    for load in loads:
        load.start()
    loads[0].wait()
    pl.semaphore_wait(barrier, shards - 1 + groups - 1)

    def grad_copy(k):
        to = lax.rem(d + k, shards)
        return pltpu.make_async_remote_copy(
            src_ref=grads_v.at[to], dst_ref=grad_in.at[k - 1],
            send_sem=grad_sems.at[0], recv_sem=grad_sems.at[1],
            device_id=(to, e), device_id_type=MESH)

    each(1, shards, lambda k: grad_copy(k).start())

    for load in loads[1:]:
        load.wait()
    m_wide[...] = mc_v[...].astype(jnp.float32)
    v_wide[...] = vc_v[...].astype(jnp.float32)

    def relay_copy(k):
        to = lax.rem(e + k, groups)
        return pltpu.make_async_remote_copy(
            src_ref=relay_out.at[k], dst_ref=relay_in.at[k - 1],
            send_sem=relay_sems.at[0], recv_sem=relay_sems.at[1],
            device_id=(d, to), device_id_type=MESH)

    for k in list(range(1, groups)) + [0]:
        to = lax.rem(e + k, groups)
        for c in range(q):
            row = order_s[0, to * q + c]
            relay_out[k, 0, c : c + 1, :] = master_v[pl.ds(row, 1), :]
            relay_out[k, 1, c : c + 1, :] = m_wide[pl.ds(row, 1), :] * ms_s[0, row]
            relay_out[k, 2, c : c + 1, :] = v_wide[pl.ds(row, 1), :] * vs_s[0, row]
        if k:
            relay_copy(k).start()

    whole = pltpu.make_async_remote_copy(
        src_ref=grad_in, dst_ref=grad_in, send_sem=grad_sems.at[0], recv_sem=grad_sems.at[1],
        device_id=(lax.rem(d + 1, shards), e), device_id_type=MESH)
    whole.wait_recv()
    gradient = grads_v[d].astype(jnp.float32)
    if shards - 1 <= UNROLL:
        for k in range(shards - 1):
            gradient = gradient + grad_in[k].astype(jnp.float32)
    else:
        gradient = lax.fori_loop(
            0, shards - 1, lambda k, g: g + grad_in[k].astype(jnp.float32), gradient)
    squares = jnp.sum(gradient * gradient, axis=0, keepdims=True)
    square_out[...] = squares

    def square_copy(k):
        flat = lax.rem(d * groups + e + k, total)
        return pltpu.make_async_remote_copy(
            src_ref=square_out, dst_ref=square_in.at[k - 1],
            send_sem=square_sems.at[0], recv_sem=square_sems.at[1],
            device_id=(flat // groups, lax.rem(flat, groups)), device_id_type=MESH)

    each(1, total, lambda k: square_copy(k).start())

    relay_whole = pltpu.make_async_remote_copy(
        src_ref=relay_in, dst_ref=relay_in, send_sem=relay_sems.at[0], recv_sem=relay_sems.at[1],
        device_id=(d, lax.rem(e + 1, groups)), device_id_type=MESH)
    relay_whole.wait_recv()
    rows = lax.broadcasted_iota(jnp.int32, (blocks, block), 0)
    placed = [jnp.zeros((blocks, block), jnp.float32) for _ in range(3)]
    for k in range(groups):
        frm = lax.rem(e - k + groups, groups)
        for c in range(q):
            here = rows == place_s[0, frm * q + c]
            for i in range(3):
                row = relay_out[0, i, c : c + 1, :] if k == 0 else relay_in[k - 1, i, c : c + 1, :]
                placed[i] = jnp.where(here, jnp.broadcast_to(row, (blocks, block)), placed[i])
    master, moment_one, moment_two = placed

    for i in range(3):
        state_out[i + 1] = placed[i]
    state_out[0] = gradient

    square_whole = pltpu.make_async_remote_copy(
        src_ref=square_in, dst_ref=square_in, send_sem=square_sems.at[0], recv_sem=square_sems.at[1],
        device_id=(lax.rem(d + 1, shards), e), device_id_type=MESH)
    square_whole.wait_recv()
    lanes_out[...] = jnp.sum(square_in[...], axis=0) + squares

    whole.wait_send()
    relay_whole.wait_send()
    square_whole.wait_send()


def update(count, state, lanes, master_out, mc_out, ms_out, vc_out, vs_out):
    gradient, master, moment_one, moment_two = (state[i] for i in range(4))
    blocks, block = gradient.shape

    total_squares = jnp.sum(lanes[...], axis=1, keepdims=True)
    root_mean = jnp.sqrt(total_squares / count + NORM_EPS)
    clip_factor = jnp.minimum(1.0, CLIP_RMS / root_mean)

    clipped = clip_factor * gradient
    m_next = BETA_ONE * moment_one + (1.0 - BETA_ONE) * clipped
    v_next = BETA_TWO * moment_two + (1.0 - BETA_TWO) * clipped * clipped
    bias_one = 1.0 - BETA_ONE**STEP
    bias_two = 1.0 - BETA_TWO**STEP
    m_mag = jnp.max(jnp.abs(m_next), axis=1, keepdims=True) + QUANT_EPS
    v_mag = jnp.max(jnp.abs(v_next), axis=1, keepdims=True) + QUANT_EPS
    step = m_next / bias_one / (jnp.sqrt(v_next / bias_two) + ADAM_EPS)
    master_out[...] = master - LEARN_RATE * (step + DECAY_RATE * master)
    mc_out[...] = (m_next / m_mag).astype(jnp.bfloat16)
    vc_out[...] = (v_next / v_mag).astype(jnp.bfloat16)
    rows = lax.broadcasted_iota(jnp.int32, (blocks, block), 0)
    diagonal = rows == lax.broadcasted_iota(jnp.int32, (blocks, block), 1)
    ms_out[...] = jnp.sum(jnp.where(diagonal, m_mag, 0.0), axis=0, keepdims=True)[:, :blocks]
    vs_out[...] = jnp.sum(jnp.where(diagonal, v_mag, 0.0), axis=0, keepdims=True)[:, :blocks]


def body(shards, groups, master_old, m_codes, m_scale, v_codes, v_scale, grad_parts, send_order, recv_place):
    blocks, block = master_old.shape[2:]
    q = blocks // groups
    f32, bf16 = jnp.float32, jnp.bfloat16
    wide = (blocks, block)
    anywhere = pl.BlockSpec(memory_space=pl.ANY)
    vmem = pl.BlockSpec(memory_space=pltpu.VMEM)
    state, lanes = pl.pallas_call(
        functools.partial(kernel, shards, groups),
        out_shape=(pltpu.VMEM((4, blocks, block), f32), pltpu.VMEM((1, block), f32)),
        in_specs=[anywhere] * 8,
        out_specs=(vmem, vmem),
        scratch_shapes=[
            pltpu.VMEM(wide, f32),
            pltpu.VMEM(wide, bf16),
            pltpu.VMEM(wide, bf16),
            pltpu.VMEM((shards, blocks, block), bf16),
            pltpu.VMEM(wide, f32),
            pltpu.VMEM(wide, f32),
            pltpu.SMEM((1, blocks), f32),
            pltpu.SMEM((1, blocks), f32),
            pltpu.SMEM((1, blocks), jnp.int32),
            pltpu.SMEM((1, blocks), jnp.int32),
            pltpu.VMEM((groups, 3, q, block), f32),
            pltpu.VMEM((groups - 1, 3, q, block), f32),
            pltpu.VMEM((shards - 1, blocks, block), bf16),
            pltpu.VMEM((1, block), f32),
            pltpu.VMEM((shards * groups - 1, 1, block), f32),
            pltpu.SemaphoreType.DMA((8,)),
            pltpu.SemaphoreType.DMA((2,)),
            pltpu.SemaphoreType.DMA((2,)),
            pltpu.SemaphoreType.DMA((2,)),
        ],
        compiler_params=pltpu.CompilerParams(collective_id=0, has_side_effects=True),
    )(
        master_old.reshape(wide), m_codes.reshape(wide), m_scale.reshape(1, blocks),
        v_codes.reshape(wide), v_scale.reshape(1, blocks),
        grad_parts.reshape(shards, blocks, block),
        send_order.reshape(1, blocks), recv_place.reshape(1, blocks),
    )
    master_new, mc, ms, vc, vs = pl.pallas_call(
        functools.partial(update, shards * groups * blocks * block),
        out_shape=(
            jax.ShapeDtypeStruct(wide, f32),
            jax.ShapeDtypeStruct(wide, bf16),
            jax.ShapeDtypeStruct((1, blocks), f32),
            jax.ShapeDtypeStruct(wide, bf16),
            jax.ShapeDtypeStruct((1, blocks), f32),
        ),
        in_specs=[vmem, vmem],
        out_specs=(vmem,) * 5,
    )(
        pltpu.with_memory_space_constraint(state, pltpu.VMEM),
        pltpu.with_memory_space_constraint(lanes, pltpu.VMEM))
    return master_new[None], mc[None], ms, vc[None], vs


def solution(mesh):
    rows = P("dp", "expert", None, None)
    flat = P("dp", "expert", None)
    return jax.shard_map(
        functools.partial(body, mesh.shape["dp"], mesh.shape["expert"]),
        mesh=mesh,
        in_specs=(rows, rows, flat, rows, flat, rows, flat, flat),
        out_specs=(
            P("expert", "dp", None),
            P("expert", "dp", None),
            P("expert", "dp"),
            P("expert", "dp", None),
            P("expert", "dp"),
        ),
        check_vma=False,
    )
```

```python
import functools

import jax
import jax.numpy as jnp
from jax import lax
from jax.experimental import pallas as pl
from jax.experimental.pallas import tpu as pltpu
from jax.sharding import PartitionSpec as P

STEP = 200

BETA_ONE = 0.9
BETA_TWO = 0.999
ADAM_EPS = 1e-08
LEARN_RATE = 0.05
DECAY_RATE = 0.1
CLIP_RMS = 1.0
QUANT_EPS = 1e-06
NORM_EPS = 1e-06

MESH = pl.DeviceIdType.MESH
UNROLL = 40


def each(first, last, step):
    if last - first <= UNROLL:
        for k in range(first, last):
            step(k)
    else:
        lax.fori_loop(first, last, lambda k, c: (step(k), c)[1], 0)


def kernel(
    shards, groups,
    master_in, mc_in, ms_in, vc_in, vs_in, grads_in, order_in, place_in,
    state_out, lanes_out,
    master_v, mc_v, vc_v, grads_v, m_wide, v_wide,
    ms_s, vs_s, order_s, place_s,
    relay_out, relay_in, grad_in, far_out, far_in, square_out, square_in, square_all,
    in_sems, grad_sems, relay_sems, far_sems, square_sems,
):
    d = lax.axis_index("dp")
    e = lax.axis_index("expert")
    blocks, block = master_v.shape
    q = blocks // groups
    half = shards // 2
    summers = half * groups
    me = d * groups + e
    lower = d < half
    upper = d >= half

    barrier = pltpu.get_barrier_semaphore()

    def greet_shard(k):
        pl.semaphore_signal(barrier, inc=1, device_id=(lax.rem(d + k, shards), e), device_id_type=MESH)

    def greet_group(k):
        pl.semaphore_signal(barrier, inc=1, device_id=(d, lax.rem(e + k, groups)), device_id_type=MESH)

    each(1, groups, greet_group)

    @pl.when(lower)
    def _():
        each(1, shards, greet_shard)

    loads = [
        pltpu.make_async_copy(src, dst, in_sems.at[i])
        for i, (src, dst) in enumerate((
            (grads_in, grads_v), (order_in, order_s), (ms_in, ms_s), (vs_in, vs_s),
            (mc_in, mc_v), (vc_in, vc_v), (master_in, master_v), (place_in, place_s),
        ))
    ]
    for load in loads:
        load.start()
    loads[0].wait()

    @pl.when(lower)
    def _():
        pl.semaphore_wait(barrier, half - 1 + groups - 1)

    @pl.when(upper)
    def _():
        pl.semaphore_wait(barrier, half + groups - 1)

    def grad_copy(p):
        return pltpu.make_async_remote_copy(
            src_ref=grads_v.at[:, p], dst_ref=grad_in.at[d],
            send_sem=grad_sems.at[0], recv_sem=grad_sems.at[1],
            device_id=(p, e), device_id_type=MESH)

    def send_grad(p):
        @pl.when(d != p)
        def _():
            grad_copy(p).start()

    each(0, half, send_grad)

    @pl.when(lower)
    def _():
        for i in range(2):
            grad_in[d, i] = grads_v[i, d]

    for load in loads[1:]:
        load.wait()
    m_wide[...] = mc_v[...].astype(jnp.float32)
    v_wide[...] = vc_v[...].astype(jnp.float32)

    def relay_copy(k):
        to = lax.rem(e + k, groups)
        return pltpu.make_async_remote_copy(
            src_ref=relay_out.at[k], dst_ref=relay_in.at[k - 1],
            send_sem=relay_sems.at[0], recv_sem=relay_sems.at[1],
            device_id=(d, to), device_id_type=MESH)

    for k in list(range(1, groups)) + [0]:
        to = lax.rem(e + k, groups)
        for c in range(q):
            row = order_s[0, to * q + c]
            relay_out[k, 0, c : c + 1, :] = master_v[pl.ds(row, 1), :]
            relay_out[k, 1, c : c + 1, :] = m_wide[pl.ds(row, 1), :] * ms_s[0, row]
            relay_out[k, 2, c : c + 1, :] = v_wide[pl.ds(row, 1), :] * vs_s[0, row]
        if k:
            relay_copy(k).start()

    def some(ref, count, sems):
        part = ref.at[pl.ds(0, count)]
        return pltpu.make_async_remote_copy(
            src_ref=part, dst_ref=part, send_sem=sems.at[0], recv_sem=sems.at[1],
            device_id=(d, lax.rem(e + 1, groups)), device_id_type=MESH)

    def far_copy():
        return pltpu.make_async_remote_copy(
            src_ref=far_out, dst_ref=far_in, send_sem=far_sems.at[0], recv_sem=far_sems.at[1],
            device_id=(lax.rem(d + half, shards), e), device_id_type=MESH)

    def square_copy(t):
        return pltpu.make_async_remote_copy(
            src_ref=square_out, dst_ref=square_in.at[me],
            send_sem=square_sems.at[0], recv_sem=square_sems.at[1],
            device_id=(t // groups, t % groups), device_id_type=MESH)

    def send_square(t):
        @pl.when(me != t)
        def _():
            square_copy(t).start()

    @pl.when(lower)
    def _():
        some(grad_in, shards - 1, grad_sems).wait_recv()
        if shards <= UNROLL:
            gradient = grad_in[0].astype(jnp.float32)
            for k in range(1, shards):
                gradient = gradient + grad_in[k].astype(jnp.float32)
        else:
            gradient = lax.fori_loop(
                0, shards, lambda k, g: g + grad_in[k].astype(jnp.float32),
                jnp.zeros((2, blocks, block), jnp.float32))
        squares = jnp.sum(gradient[0] * gradient[0] + gradient[1] * gradient[1], axis=0, keepdims=True)
        square_out[...] = squares
        square_in[me] = squares
        far_out[...] = gradient[1]
        state_out[0] = gradient[0]
        each(0, shards * groups, send_square)
        far_copy().start()

    relay_whole = some(relay_in, groups - 1, relay_sems)
    relay_whole.wait_recv()
    rows = lax.broadcasted_iota(jnp.int32, (blocks, block), 0)
    placed = [jnp.zeros((blocks, block), jnp.float32) for _ in range(3)]
    for k in range(groups):
        frm = lax.rem(e - k + groups, groups)
        for c in range(q):
            here = rows == place_s[0, frm * q + c]
            for i in range(3):
                row = relay_out[0, i, c : c + 1, :] if k == 0 else relay_in[k - 1, i, c : c + 1, :]
                placed[i] = jnp.where(here, jnp.broadcast_to(row, (blocks, block)), placed[i])
    for i in range(3):
        state_out[i + 1] = placed[i]

    @pl.when(lower)
    def _():
        some(square_in, summers - 1, square_sems).wait_recv()

    @pl.when(upper)
    def _():
        far_copy().wait_recv()
        state_out[0] = far_in[...]
        some(square_in, summers, square_sems).wait_recv()

    lanes_out[...] = jnp.sum(square_in[...], axis=0)

    relay_whole.wait_send()

    @pl.when(lower)
    def _():
        some(grad_in, half - 1, grad_sems).wait_send()
        far_copy().wait_send()
        some(square_all, shards * groups - 1, square_sems).wait_send()

    @pl.when(upper)
    def _():
        some(grad_in, half, grad_sems).wait_send()


def update(count, state, lanes, master_out, mc_out, ms_out, vc_out, vs_out):
    gradient, master, moment_one, moment_two = (state[i] for i in range(4))
    blocks, block = gradient.shape

    total_squares = jnp.sum(lanes[...], axis=1, keepdims=True)
    root_mean = jnp.sqrt(total_squares / count + NORM_EPS)
    clip_factor = jnp.minimum(1.0, CLIP_RMS / root_mean)

    clipped = clip_factor * gradient
    m_next = BETA_ONE * moment_one + (1.0 - BETA_ONE) * clipped
    v_next = BETA_TWO * moment_two + (1.0 - BETA_TWO) * clipped * clipped
    bias_one = 1.0 - BETA_ONE**STEP
    bias_two = 1.0 - BETA_TWO**STEP
    m_mag = jnp.max(jnp.abs(m_next), axis=1, keepdims=True) + QUANT_EPS
    v_mag = jnp.max(jnp.abs(v_next), axis=1, keepdims=True) + QUANT_EPS
    step = m_next / bias_one / (jnp.sqrt(v_next / bias_two) + ADAM_EPS)
    master_out[...] = master - LEARN_RATE * (step + DECAY_RATE * master)
    mc_out[...] = (m_next / m_mag).astype(jnp.bfloat16)
    vc_out[...] = (v_next / v_mag).astype(jnp.bfloat16)
    rows = lax.broadcasted_iota(jnp.int32, (blocks, block), 0)
    diagonal = rows == lax.broadcasted_iota(jnp.int32, (blocks, block), 1)
    ms_out[...] = jnp.sum(jnp.where(diagonal, m_mag, 0.0), axis=0, keepdims=True)[:, :blocks]
    vs_out[...] = jnp.sum(jnp.where(diagonal, v_mag, 0.0), axis=0, keepdims=True)[:, :blocks]


def body(shards, groups, master_old, m_codes, m_scale, v_codes, v_scale, grad_parts, send_order, recv_place):
    blocks, block = master_old.shape[2:]
    q = blocks // groups
    f32, bf16 = jnp.float32, jnp.bfloat16
    wide = (blocks, block)
    anywhere = pl.BlockSpec(memory_space=pl.ANY)
    vmem = pl.BlockSpec(memory_space=pltpu.VMEM)
    state, lanes = pl.pallas_call(
        functools.partial(kernel, shards, groups),
        out_shape=(pltpu.VMEM((4, blocks, block), f32), pltpu.VMEM((1, block), f32)),
        in_specs=[anywhere] * 8,
        out_specs=(vmem, vmem),
        scratch_shapes=[
            pltpu.VMEM(wide, f32),
            pltpu.VMEM(wide, bf16),
            pltpu.VMEM(wide, bf16),
            pltpu.VMEM((2, shards // 2, blocks, block), bf16),
            pltpu.VMEM(wide, f32),
            pltpu.VMEM(wide, f32),
            pltpu.SMEM((1, blocks), f32),
            pltpu.SMEM((1, blocks), f32),
            pltpu.SMEM((1, blocks), jnp.int32),
            pltpu.SMEM((1, blocks), jnp.int32),
            pltpu.VMEM((groups, 3, q, block), f32),
            pltpu.VMEM((groups - 1, 3, q, block), f32),
            pltpu.VMEM((shards, 2, blocks, block), bf16),
            pltpu.VMEM(wide, f32),
            pltpu.VMEM(wide, f32),
            pltpu.VMEM((1, block), f32),
            pltpu.VMEM((shards // 2 * groups, 1, block), f32),
            pltpu.VMEM((shards * groups - 1, 1, block), f32),
            pltpu.SemaphoreType.DMA((8,)),
            pltpu.SemaphoreType.DMA((2,)),
            pltpu.SemaphoreType.DMA((2,)),
            pltpu.SemaphoreType.DMA((2,)),
            pltpu.SemaphoreType.DMA((2,)),
        ],
        compiler_params=pltpu.CompilerParams(collective_id=0, has_side_effects=True),
    )(
        master_old.reshape(wide), m_codes.reshape(wide), m_scale.reshape(1, blocks),
        v_codes.reshape(wide), v_scale.reshape(1, blocks),
        grad_parts.reshape(2, shards // 2, blocks, block),
        send_order.reshape(1, blocks), recv_place.reshape(1, blocks),
    )
    master_new, mc, ms, vc, vs = pl.pallas_call(
        functools.partial(update, shards * groups * blocks * block),
        out_shape=(
            jax.ShapeDtypeStruct(wide, f32),
            jax.ShapeDtypeStruct(wide, bf16),
            jax.ShapeDtypeStruct((1, blocks), f32),
            jax.ShapeDtypeStruct(wide, bf16),
            jax.ShapeDtypeStruct((1, blocks), f32),
        ),
        in_specs=[vmem, vmem],
        out_specs=(vmem,) * 5,
    )(
        pltpu.with_memory_space_constraint(state, pltpu.VMEM),
        pltpu.with_memory_space_constraint(lanes, pltpu.VMEM))
    return master_new[None], mc[None], ms, vc[None], vs


def solution(mesh):
    rows = P("dp", "expert", None, None)
    flat = P("dp", "expert", None)
    return jax.shard_map(
        functools.partial(body, mesh.shape["dp"], mesh.shape["expert"]),
        mesh=mesh,
        in_specs=(rows, rows, flat, rows, flat, rows, flat, flat),
        out_specs=(
            P("expert", "dp", None),
            P("expert", "dp", None),
            P("expert", "dp"),
            P("expert", "dp", None),
            P("expert", "dp"),
        ),
        check_vma=False,
    )
```

```python
import functools

import jax
import jax.numpy as jnp
from jax import lax
from jax.experimental import pallas as pl
from jax.experimental.pallas import tpu as pltpu
from jax.sharding import PartitionSpec as P

STEP = 200

BETA_ONE = 0.9
BETA_TWO = 0.999
ADAM_EPS = 1e-08
LEARN_RATE = 0.05
DECAY_RATE = 0.1
CLIP_RMS = 1.0
QUANT_EPS = 1e-06
NORM_EPS = 1e-06

MESH = pl.DeviceIdType.MESH
UNROLL = 40
SECTIONS = 8


def each(first, last, step):
    if last - first <= UNROLL:
        for k in range(first, last):
            step(k)
    else:
        lax.fori_loop(first, last, lambda k, c: (step(k), c)[1], 0)


def kernel(
    shards, groups,
    master_in, mc_in, ms_in, vc_in, vs_in, grads_in, order_in, place_in,
    state_out, lanes_out,
    master_v, mc_v, vc_v, m_wide, v_wide,
    ms_s, vs_s, order_s, place_s,
    relay_out, relay_in, grad_in, far_out, far_in, square_out, square_in, square_all,
    in_sems, grad_sems, relay_sems, far_sems, square_sems,
):
    d = lax.axis_index("dp")
    e = lax.axis_index("expert")
    blocks, block = master_v.shape
    q = blocks // groups
    part = shards // SECTIONS
    summers = part * groups
    me = d * groups + e
    lower = d < part
    upper = d >= part

    barrier = pltpu.get_barrier_semaphore()

    def greet_shard(k):
        pl.semaphore_signal(barrier, inc=1, device_id=(lax.rem(d + k, shards), e), device_id_type=MESH)

    def greet_group(k):
        pl.semaphore_signal(barrier, inc=1, device_id=(d, lax.rem(e + k, groups)), device_id_type=MESH)

    each(1, groups, greet_group)

    @pl.when(lower)
    def _():
        each(1, shards, greet_shard)

    loads = [
        pltpu.make_async_copy(src, dst, in_sems.at[i])
        for i, (src, dst) in enumerate((
            (order_in, order_s), (ms_in, ms_s), (vs_in, vs_s),
            (mc_in, mc_v), (vc_in, vc_v), (master_in, master_v), (place_in, place_s),
        ))
    ]
    for load in loads:
        load.start()

    @pl.when(lower)
    def _():
        pl.semaphore_wait(barrier, part - 1 + groups - 1)

    @pl.when(upper)
    def _():
        pl.semaphore_wait(barrier, part + groups - 1)

    def grad_copy(p):
        return pltpu.make_async_remote_copy(
            src_ref=grads_in.at[:, p], dst_ref=grad_in.at[d],
            send_sem=grad_sems.at[0], recv_sem=grad_sems.at[1],
            device_id=(p, e), device_id_type=MESH)

    def send_grad(p):
        @pl.when(d != p)
        def _():
            grad_copy(p).start()

    each(0, part, send_grad)

    def own_grad():
        return pltpu.make_async_copy(grads_in.at[:, d], grad_in.at[d], in_sems.at[7])

    @pl.when(lower)
    def _():
        own_grad().start()

    for load in loads:
        load.wait()
    m_wide[...] = mc_v[...].astype(jnp.float32)
    v_wide[...] = vc_v[...].astype(jnp.float32)

    def relay_copy(k):
        to = lax.rem(e + k, groups)
        return pltpu.make_async_remote_copy(
            src_ref=relay_out.at[k], dst_ref=relay_in.at[k - 1],
            send_sem=relay_sems.at[0], recv_sem=relay_sems.at[1],
            device_id=(d, to), device_id_type=MESH)

    for k in list(range(1, groups)) + [0]:
        to = lax.rem(e + k, groups)
        for c in range(q):
            row = order_s[0, to * q + c]
            relay_out[k, 0, c : c + 1, :] = master_v[pl.ds(row, 1), :]
            relay_out[k, 1, c : c + 1, :] = m_wide[pl.ds(row, 1), :] * ms_s[0, row]
            relay_out[k, 2, c : c + 1, :] = v_wide[pl.ds(row, 1), :] * vs_s[0, row]
        if k:
            relay_copy(k).start()

    def some(ref, count, sems):
        part = ref.at[pl.ds(0, count)]
        return pltpu.make_async_remote_copy(
            src_ref=part, dst_ref=part, send_sem=sems.at[0], recv_sem=sems.at[1],
            device_id=(d, lax.rem(e + 1, groups)), device_id_type=MESH)

    def far_copy(i):
        return pltpu.make_async_remote_copy(
            src_ref=far_out.at[i - 1], dst_ref=far_in.at[0],
            send_sem=far_sems.at[0], recv_sem=far_sems.at[1],
            device_id=(lax.rem(d + i * part, shards), e), device_id_type=MESH)

    def square_copy(t):
        return pltpu.make_async_remote_copy(
            src_ref=square_out, dst_ref=square_in.at[me],
            send_sem=square_sems.at[0], recv_sem=square_sems.at[1],
            device_id=(t // groups, t % groups), device_id_type=MESH)

    def send_square(t):
        @pl.when(me != t)
        def _():
            square_copy(t).start()

    @pl.when(lower)
    def _():
        own_grad().wait()
        some(grad_in, shards - 1, grad_sems).wait_recv()
        if shards <= UNROLL:
            gradient = grad_in[0].astype(jnp.float32)
            for k in range(1, shards):
                gradient = gradient + grad_in[k].astype(jnp.float32)
        else:
            gradient = lax.fori_loop(
                0, shards, lambda k, g: g + grad_in[k].astype(jnp.float32),
                jnp.zeros((SECTIONS, blocks, block), jnp.float32))
        squares = jnp.sum(jnp.sum(gradient * gradient, axis=0), axis=0, keepdims=True)
        square_out[...] = squares
        square_in[me] = squares
        far_out[...] = gradient[1:]
        state_out[0] = gradient[0]
        each(0, shards * groups, send_square)
        for i in range(1, SECTIONS):
            far_copy(i).start()

    relay_whole = some(relay_in, groups - 1, relay_sems)
    relay_whole.wait_recv()
    rows = lax.broadcasted_iota(jnp.int32, (blocks, block), 0)
    placed = [jnp.zeros((blocks, block), jnp.float32) for _ in range(3)]
    for k in range(groups):
        frm = lax.rem(e - k + groups, groups)
        for c in range(q):
            here = rows == place_s[0, frm * q + c]
            for i in range(3):
                row = relay_out[0, i, c : c + 1, :] if k == 0 else relay_in[k - 1, i, c : c + 1, :]
                placed[i] = jnp.where(here, jnp.broadcast_to(row, (blocks, block)), placed[i])
    for i in range(3):
        state_out[i + 1] = placed[i]

    @pl.when(lower)
    def _():
        some(square_in, summers - 1, square_sems).wait_recv()

    @pl.when(upper)
    def _():
        far_copy(1).wait_recv()
        state_out[0] = far_in[0]
        some(square_in, summers, square_sems).wait_recv()

    lanes_out[...] = jnp.sum(square_in[...], axis=0)

    relay_whole.wait_send()

    @pl.when(lower)
    def _():
        some(grad_in, part - 1, grad_sems).wait_send()
        some(far_out, SECTIONS - 1, far_sems).wait_send()
        some(square_all, shards * groups - 1, square_sems).wait_send()

    @pl.when(upper)
    def _():
        some(grad_in, part, grad_sems).wait_send()


def update(count, state, lanes, master_out, mc_out, ms_out, vc_out, vs_out):
    gradient, master, moment_one, moment_two = (state[i] for i in range(4))
    blocks, block = gradient.shape

    total_squares = jnp.sum(lanes[...], axis=1, keepdims=True)
    root_mean = jnp.sqrt(total_squares / count + NORM_EPS)
    clip_factor = jnp.minimum(1.0, CLIP_RMS / root_mean)

    clipped = clip_factor * gradient
    m_next = BETA_ONE * moment_one + (1.0 - BETA_ONE) * clipped
    v_next = BETA_TWO * moment_two + (1.0 - BETA_TWO) * clipped * clipped
    bias_one = 1.0 - BETA_ONE**STEP
    bias_two = 1.0 - BETA_TWO**STEP
    m_mag = jnp.max(jnp.abs(m_next), axis=1, keepdims=True) + QUANT_EPS
    v_mag = jnp.max(jnp.abs(v_next), axis=1, keepdims=True) + QUANT_EPS
    step = m_next / bias_one / (jnp.sqrt(v_next / bias_two) + ADAM_EPS)
    master_out[...] = master - LEARN_RATE * (step + DECAY_RATE * master)
    mc_out[...] = (m_next / m_mag).astype(jnp.bfloat16)
    vc_out[...] = (v_next / v_mag).astype(jnp.bfloat16)
    rows = lax.broadcasted_iota(jnp.int32, (blocks, block), 0)
    diagonal = rows == lax.broadcasted_iota(jnp.int32, (blocks, block), 1)
    ms_out[...] = jnp.sum(jnp.where(diagonal, m_mag, 0.0), axis=0, keepdims=True)[:, :blocks]
    vs_out[...] = jnp.sum(jnp.where(diagonal, v_mag, 0.0), axis=0, keepdims=True)[:, :blocks]


def body(shards, groups, master_old, m_codes, m_scale, v_codes, v_scale, grad_parts, send_order, recv_place):
    blocks, block = master_old.shape[2:]
    q = blocks // groups
    f32, bf16 = jnp.float32, jnp.bfloat16
    wide = (blocks, block)
    anywhere = pl.BlockSpec(memory_space=pl.ANY)
    vmem = pl.BlockSpec(memory_space=pltpu.VMEM)
    state, lanes = pl.pallas_call(
        functools.partial(kernel, shards, groups),
        out_shape=(pltpu.VMEM((4, blocks, block), f32), pltpu.VMEM((1, block), f32)),
        in_specs=[anywhere] * 8,
        out_specs=(vmem, vmem),
        scratch_shapes=[
            pltpu.VMEM(wide, f32),
            pltpu.VMEM(wide, bf16),
            pltpu.VMEM(wide, bf16),
            pltpu.VMEM(wide, f32),
            pltpu.VMEM(wide, f32),
            pltpu.SMEM((1, blocks), f32),
            pltpu.SMEM((1, blocks), f32),
            pltpu.SMEM((1, blocks), jnp.int32),
            pltpu.SMEM((1, blocks), jnp.int32),
            pltpu.VMEM((groups, 3, q, block), f32),
            pltpu.VMEM((groups - 1, 3, q, block), f32),
            pltpu.VMEM((shards, SECTIONS, blocks, block), bf16),
            pltpu.VMEM((SECTIONS - 1, blocks, block), f32),
            pltpu.VMEM((1, blocks, block), f32),
            pltpu.VMEM((1, block), f32),
            pltpu.VMEM((shards // SECTIONS * groups, 1, block), f32),
            pltpu.VMEM((shards * groups - 1, 1, block), f32),
            pltpu.SemaphoreType.DMA((8,)),
            pltpu.SemaphoreType.DMA((2,)),
            pltpu.SemaphoreType.DMA((2,)),
            pltpu.SemaphoreType.DMA((2,)),
            pltpu.SemaphoreType.DMA((2,)),
        ],
        compiler_params=pltpu.CompilerParams(collective_id=0, has_side_effects=True),
    )(
        master_old.reshape(wide), m_codes.reshape(wide), m_scale.reshape(1, blocks),
        v_codes.reshape(wide), v_scale.reshape(1, blocks),
        grad_parts.reshape(SECTIONS, shards // SECTIONS, blocks, block),
        send_order.reshape(1, blocks), recv_place.reshape(1, blocks),
    )
    master_new, mc, ms, vc, vs = pl.pallas_call(
        functools.partial(update, shards * groups * blocks * block),
        out_shape=(
            jax.ShapeDtypeStruct(wide, f32),
            jax.ShapeDtypeStruct(wide, bf16),
            jax.ShapeDtypeStruct((1, blocks), f32),
            jax.ShapeDtypeStruct(wide, bf16),
            jax.ShapeDtypeStruct((1, blocks), f32),
        ),
        in_specs=[vmem, vmem],
        out_specs=(vmem,) * 5,
    )(
        pltpu.with_memory_space_constraint(state, pltpu.VMEM),
        pltpu.with_memory_space_constraint(lanes, pltpu.VMEM))
    return master_new[None], mc[None], ms, vc[None], vs


def solution(mesh):
    rows = P("dp", "expert", None, None)
    flat = P("dp", "expert", None)
    return jax.shard_map(
        functools.partial(body, mesh.shape["dp"], mesh.shape["expert"]),
        mesh=mesh,
        in_specs=(rows, rows, flat, rows, flat, rows, flat, flat),
        out_specs=(
            P("expert", "dp", None),
            P("expert", "dp", None),
            P("expert", "dp"),
            P("expert", "dp", None),
            P("expert", "dp"),
        ),
        check_vma=False,
    )
```
